128 devices in a mesh: ka: 16 (over x_lo, z, core), aux: 8 (over x_hi, y).
Axes of the slice: x: 4 (x_hi: 2, x_lo: 2; x = x_hi * 2 + x_lo), y: 4, z: 4, core: 2. Of those that a mesh axis runs over, the one named last changes fastest.
Arguments:
- orbital_coef: bfloat16 [2, 16, 192, 128], P(None, 'ka'), may hold values from -0.4375 to 0.4375
- dftensor: bfloat16 [2, 16, 192, 192, 1024], P(None, 'ka', None, None, 'aux'), may hold values from -1.5 to 1.5
- shifted_index: int32 [16], replicated, may hold values from 0 to 15, each once
Outputs:
- integrals: float32 [2, 16384, 1024], P(None, 'ka', 'aux')
The draws below stay inside these ranges and needn't reach their ends.
Inputs may be any that keep to these rules, and one draw needn't show every extreme that they name: `shifted_index`: a permutation of the 16 k-points.
All inputs are finite; a program needn't handle non-finite values.
Results may differ from the reference program's by a relative error of at most 0.004.
Values may be sent and summed in bfloat16 or wider, within the bound.
A program may use at most 192 MiB of HBM per device.

```python
import jax
import jax.numpy as jnp
from jax import lax

NAO = 192
NEMB = 128
NK = 16
NAUX = 1024
NPAIR = 16384
PANEL = 1024
N_KA = 16


def block_levels(own_key, shape, cuts, low, top_value):
    def one(dim, parts):
        heights = jax.random.uniform(jax.random.fold_in(jax.random.fold_in(own_key, 6), dim), (parts,), jnp.float32, low / len(cuts), top_value / len(cuts))
        return jnp.repeat(jnp.exp(heights), shape[dim] // parts).reshape((-1,) + (1,) * (len(shape) - dim - 1))

    level = one(*cuts[0])
    for cut in cuts[1:]:
        level = level * one(*cut)
    return level


def gaussian(rng, shape, width, reach, shards=(), held_as=jnp.bfloat16):
    factor_of = block_levels(rng, shape, shards, -0.22, 0.18) if shards else 1.0
    drawn = jax.random.normal(rng, shape, jnp.float32) * width * factor_of
    return jnp.minimum(jnp.maximum(drawn, -reach), reach).astype(held_as)


def setup_inputs(seed: int = 0) -> dict:
    splits = jax.random.split(jax.random.key(seed), 4)
    return {
        "orbital_coef": gaussian(splits[0], (2, NK, NAO, NEMB), NAO ** -0.5, 0.4375, ((1, 16),)),
        "dftensor": gaussian(splits[1], (2, NK, NAO, NAO, NAUX), 16 ** -0.5, 1.5, ((1, 16), (4, 8))),
        "shifted_index": jax.random.permutation(splits[2], NK).astype(jnp.int32),
    }


def transform_pair(coef_left, coef_right, tensor):
    left_real = coef_left[0].astype(jnp.float32)
    left_imag = coef_left[1].astype(jnp.float32)
    right_real = coef_right[0].astype(jnp.float32)
    right_imag = coef_right[1].astype(jnp.float32)
    tensor_real = tensor[0].astype(jnp.float32)
    tensor_imag = tensor[1].astype(jnp.float32)
    half_real = jnp.einsum('ma,mnp->anp', left_real, tensor_real) + jnp.einsum('ma,mnp->anp', left_imag, tensor_imag)
    half_imag = jnp.einsum('ma,mnp->anp', left_real, tensor_imag) - jnp.einsum('ma,mnp->anp', left_imag, tensor_real)
    half_real = half_real.astype(jnp.bfloat16).astype(jnp.float32)
    half_imag = half_imag.astype(jnp.bfloat16).astype(jnp.float32)
    pair_real = jnp.einsum('anp,nb->pab', half_real, right_real) - jnp.einsum('anp,nb->pab', half_imag, right_imag)
    pair_imag = jnp.einsum('anp,nb->pab', half_real, right_imag) + jnp.einsum('anp,nb->pab', half_imag, right_real)
    return jnp.stack([pair_real, pair_imag])


def eri_tile(row_data, column_data):
    contract_dims = (((0,), (0,)), ((), ()))
    real_part = lax.dot_general(row_data[0], column_data[0], contract_dims, preferred_element_type=jnp.float32)
    real_part = real_part + lax.dot_general(row_data[1], column_data[1], contract_dims, preferred_element_type=jnp.float32)
    imag_part = lax.dot_general(row_data[1], column_data[0], contract_dims, preferred_element_type=jnp.float32)
    imag_part = imag_part - lax.dot_general(row_data[0], column_data[1], contract_dims, preferred_element_type=jnp.float32)
    return jnp.stack([real_part, imag_part])


def reference(orbital_coef, dftensor, shifted_index):
    def add_kpoint(running, kpoint):
        coef_left = lax.dynamic_index_in_dim(orbital_coef, kpoint, 1, False)
        coef_right = lax.dynamic_index_in_dim(orbital_coef, shifted_index[kpoint].astype(jnp.int32), 1, False)
        tensor = lax.dynamic_index_in_dim(dftensor, kpoint, 1, False)
        return running + transform_pair(coef_left, coef_right, tensor), None

    initial = jnp.zeros((2, NAUX, NEMB, NEMB), jnp.float32)
    summed, _ = lax.scan(add_kpoint, initial, jnp.arange(NK, dtype=jnp.int32))
    fitted = (summed / NK).astype(jnp.bfloat16).reshape(2, NAUX, N_KA, PANEL)
    panels = jnp.moveaxis(fitted, 2, 0)
    tiles = lax.map(lambda panel_data: eri_tile(panel_data, panel_data), panels)
    return jnp.moveaxis(tiles, 0, 1).reshape(2, NPAIR, PANEL)
```

```python
import functools

import jax
import jax.numpy as jnp
from jax import lax
from jax.experimental import pallas as pl
from jax.experimental.pallas import tpu as pltpu
from jax.sharding import PartitionSpec as P

F32, BF16 = jnp.float32, jnp.bfloat16
MESH = pl.DeviceIdType.MESH
ROWS = 16
CHUNKS = 4
CORES, ZS, XS, YS = 2, 4, 2, 4


def matmul(left, right):
    return lax.dot_general(left, right, (((1,), (0,)), ((), ())), preferred_element_type=F32)


def matmul_nt(left, right):
    return lax.dot_general(left, right, (((1,), (1,)), ((), ())), preferred_element_type=F32)


def kernel(coef, tensor, index, out, blocks, w1, w2, half, cg, cs, away, mine, other, za, zb, zm, zp, xr, fg, cols,
           lsem, gsend, grecv, dsend, drecv, local_sem):
    nao = coef.shape[2]
    part = nao // YS
    nblocks = nao // ROWS
    ka, aux = lax.axis_index("ka"), lax.axis_index("aux")
    core, z, x = lax.rem(ka, CORES), lax.rem(lax.div(ka, CORES), ZS), lax.div(ka, CORES * ZS)
    y, xh = lax.rem(aux, YS), lax.div(aux, YS)
    up, down, across = lax.rem(z + 1, ZS), lax.rem(z + ZS - 1, ZS), lax.rem(z + 2, ZS)
    y_up, y_down = lax.rem(y + 1, YS), lax.rem(y + YS - 1, YS)
    aux_far = lax.rem(aux + YS, 2 * YS)
    to_core = (ka + 1 - 2 * core, aux)
    to_x = (lax.rem(ka + CORES * ZS, XS * CORES * ZS), aux)
    to_up = (x * CORES * ZS + up * CORES + core, aux)
    to_down = (x * CORES * ZS + down * CORES + core, aux)
    to_y_up, to_y_down = (ka, xh * YS + y_up), (ka, xh * YS + y_down)
    to_far = (ka, aux_far)
    x_other = 1 - x

    def load(i):
        return pltpu.make_async_copy(tensor.at[:, :, pl.ds(pl.multiple_of(i * ROWS, ROWS), ROWS), :], blocks.at[i], lsem.at[i])

    for i in range(nblocks):
        load(i).start()

    barrier = pltpu.get_barrier_semaphore()
    for partner in (to_core, to_x, to_up, to_down, to_y_up, to_y_down, to_far):
        pl.semaphore_signal(barrier, inc=1, device_id=partner, device_id_type=MESH)
    pl.semaphore_wait(barrier, 7)

    def send(src, dst, send_sem, recv_sem, where):
        return pltpu.make_async_remote_copy(
            src_ref=src, dst_ref=dst, send_sem=send_sem, recv_sem=recv_sem, device_id=where, device_id_type=MESH
        )

    slot = z * 4 + x * 2 + core
    own_rows = coef.at[:, 0, pl.ds(pl.multiple_of(y * part, 16), part), :]
    keep = pltpu.make_async_copy(own_rows, cg.at[slot], local_sem)

    def gather(n):
        def one(src, dst, where):
            return send(src, dst, gsend.at[n], grecv.at[n], where)

        if n == 0:
            return one(own_rows, cg.at[slot], to_core)
        if n == 1:
            rows = cg.at[pl.ds(z * 4 + x * 2, 2)]
            return one(rows, rows, to_x)
        if n in (2, 3):
            rows = cg.at[pl.ds(z * 4, 4)]
            return one(rows, rows, to_up if n == 2 else to_down)
        if n == 4:
            rows = cg.at[pl.ds(down * 4, 4)]
            return one(rows, rows, to_up)
        if n in (5, 6):
            return one(cs.at[y], cs.at[y], to_y_up if n == 5 else to_y_down)
        return one(cs.at[y_down], cs.at[y_down], to_y_up)

    keep.start()
    gather(0).start()

    left_real, left_imag = coef[0, 0], coef[1, 0]
    w1[...] = jnp.concatenate(
        [jnp.concatenate([left_real, -left_imag], 1), jnp.concatenate([left_imag, left_real], 1)], 0
    ).T

    def first(i, carry):
        @pl.when(i == 1)
        def _():
            keep.wait()
            gather(0).wait()
            gather(1).start()

        @pl.when(i == 3)
        def _():
            gather(1).wait()
            gather(2).start()
            gather(3).start()

        @pl.when(i == 6)
        def _():
            gather(2).wait()
            gather(3).wait()
            gather(4).start()

        @pl.when(i == 9)
        def _():
            gather(4).wait()
            wanted = index[ka]
            picked = lax.rem(lax.div(wanted, 2), 4) * 4 + lax.div(wanted, 8) * 2 + lax.rem(wanted, 2)
            cs[y] = cg[picked]
            gather(5).start()
            gather(6).start()

        load(i).wait()
        block = jnp.swapaxes(blocks[i].reshape(2 * nao, ROWS, 128), 0, 1)
        halves = []
        for n in range(0, ROWS, 2):
            got = matmul(w1[...], jnp.concatenate([block[n], block[n + 1]], 1)).astype(BF16)
            halves += [got[:, :128], got[:, 128:]]
        half[:, pl.ds(pl.multiple_of(i * ROWS, ROWS), ROWS), :] = jnp.swapaxes(jnp.stack(halves), 0, 1)
        return carry

    lax.fori_loop(0, nblocks, first, 0)

    gather(5).wait()
    gather(6).wait()
    gather(7).start()
    gather(7).wait()
    right_real = jnp.concatenate([cs[n, 0] for n in range(YS)], 0)
    right_imag = jnp.concatenate([cs[n, 1] for n in range(YS)], 0)
    w2[...] = jnp.concatenate(
        [jnp.concatenate([right_real, right_imag], 1), jnp.concatenate([-right_imag, right_real], 1)], 0
    ).T

    def pairs(c, target, into):
        def one(q, carry):
            a = 8 * (lax.rem(q, 2) * 8 + lax.div(q, 2) * 2 + target) + 2 * c
            sides = [jnp.concatenate([half[a + n], half[128 + a + n]], 0) for n in range(2)]
            got = matmul(w2[...], jnp.concatenate(sides, 1)).astype(BF16)
            into[c, q, 0] = got[:, :128]
            into[c, q, 1] = got[:, 128:]
            return carry

        lax.fori_loop(0, 8, one, 0)

    def add(dst, srcs, scale=None):
        def one(i, carry):
            at = (lax.div(i, 4), pl.ds(pl.multiple_of(lax.rem(i, 4) * 64, 64), 64))
            total = srcs[0][at].astype(F32)
            for src in srcs[1:]:
                total = total + src[at].astype(F32)
            if scale is not None:
                total = total * scale
            dst[at] = total.astype(BF16)
            return carry

        lax.fori_loop(0, 8, one, 0)

    def move(kind, c):
        def one(src, dst, where):
            return send(src, dst, dsend.at[kind, c], drecv.at[kind, c], where)

        if kind == 0:
            return one(away.at[c], other.at[c], to_core)
        if kind == 1:
            return one(mine.at[c, across * 2], za.at[c], to_up)
        if kind == 2:
            return one(mine.at[c, across * 2 + 1], zb.at[c], to_down)
        if kind in (3, 5):
            n = 1 if kind == 3 else 0
            return one(mine.at[c, up * 2 + n], zm.at[c, n], to_up)
        if kind in (4, 6):
            n = 0 if kind == 4 else 1
            return one(mine.at[c, down * 2 + n], zp.at[c, n], to_down)
        if kind == 7:
            return one(mine.at[c, z * 2 + x_other], xr.at[c], to_x)
        if kind == 8:
            return one(fg.at[aux, c], fg.at[aux, c], to_far)
        if kind in (9, 10):
            return one(fg.at[aux, c], fg.at[aux, c], to_y_up if kind == 9 else to_y_down)
        if kind in (11, 12):
            return one(fg.at[aux_far, c], fg.at[aux_far, c], to_y_up if kind == 11 else to_y_down)
        base = (xh if kind < 15 else 1 - xh) * YS
        if kind in (13, 15):
            piece = fg.at[base + y_down, c, 0]
            return one(piece, piece, to_y_up)
        piece = fg.at[base + y_up, c, 1]
        return one(piece, piece, to_y_down)

    def stage_a(c):
        pairs(c, 1 - core, away)
        move(0, c).start()
        pairs(c, core, mine)
        move(0, c).wait_recv()
        for kind, q in ((1, across * 2), (2, across * 2 + 1)):
            add(mine.at[c, q], (mine.at[c, q], other.at[c, q]))
            move(kind, c).start()

    def stage_a2(c):
        for kind, q in ((3, up * 2 + 1), (4, down * 2)):
            add(mine.at[c, q], (mine.at[c, q], other.at[c, q]))
            move(kind, c).start()

    def stage_b(c):
        for first_kind, kind, q, got in ((1, 5, up * 2, za), (2, 6, down * 2 + 1, zb)):
            move(first_kind, c).wait_recv()
            add(mine.at[c, q], (mine.at[c, q], other.at[c, q], got.at[c]))
            move(kind, c).start()

    def stage_d(c):
        for kind in (3, 4, 5, 6):
            move(kind, c).wait_recv()
        q = z * 2 + x_other
        add(mine.at[c, q], (mine.at[c, q], other.at[c, q], zm.at[c, x_other], zp.at[c, x_other]))
        move(7, c).start()

    def stage_e(c):
        move(7, c).wait_recv()
        q = z * 2 + x
        add(fg.at[aux, c], (mine.at[c, q], other.at[c, q], zm.at[c, x], zp.at[c, x], xr.at[c]), 1 / (CORES * ZS * XS))
        for kind in (8, 9, 10):
            move(kind, c).start()

    def stage_g(c):
        move(8, c).wait_recv()
        move(11, c).start()
        move(12, c).start()

    def stage_h(c):
        for wait_kind, kind in ((9, 13), (10, 14), (11, 15), (12, 16)):
            move(wait_kind, c).wait_recv()
            move(kind, c).start()

    def stage_i(c):
        for kind in (13, 14, 15, 16):
            move(kind, c).wait_recv()

    stage_a(0)
    stage_a(1)
    stage_a2(0)
    stage_b(0)
    stage_a(2)
    stage_a2(1)
    stage_b(1)
    stage_a(3)
    stage_d(0)
    stage_a2(2)
    stage_b(2)
    stage_d(1)
    stage_e(0)
    stage_a2(3)
    stage_b(3)
    stage_g(0)
    stage_d(2)
    stage_e(1)
    stage_h(0)
    stage_g(1)
    stage_d(3)
    stage_e(2)
    stage_h(1)
    stage_g(2)
    stage_e(3)
    stage_h(2)
    stage_g(3)
    stage_h(3)
    for c in range(CHUNKS):
        stage_i(c)

    col_chunk, col_part = lax.div(aux, 2), lax.rem(aux, 2)
    for j in range(2 * YS):
        column = fg[j, col_chunk, col_part]
        real, imag = column[:128], column[128:]
        cols[j] = jnp.concatenate(
            [jnp.concatenate([real, imag], 1), jnp.concatenate([-imag, real], 1)], 0
        )

    def tile(c, carry):
        total = jnp.zeros((256, 256), F32)
        for j in range(2 * YS):
            rows = jnp.concatenate(
                [jnp.concatenate([fg[j, c, n, :128], fg[j, c, n, 128:]], 1) for n in range(2)], 0
            )
            total = total + matmul_nt(rows, cols[j])
        at = pl.ds(pl.multiple_of(c * 256, 256), 256)
        out[0, at, :] = total[:, :128]
        out[1, at, :] = total[:, 128:]
        return carry

    lax.fori_loop(0, CHUNKS, tile, 0)

    for kind in range(17):
        for c in range(CHUNKS):
            move(kind, c).wait_send()


def local(orbital_coef, dftensor, shifted_index):
    nao, nemb = orbital_coef.shape[2:]
    depth = dftensor.shape[-1]
    tensor = dftensor.reshape(2, nao, nao, depth)
    unit = (2, 2 * nemb, depth)
    return pl.pallas_call(
        kernel,
        out_shape=jax.ShapeDtypeStruct((2, 8 * nemb, nemb), F32),
        in_specs=[
            pl.BlockSpec(memory_space=pltpu.VMEM),
            pl.BlockSpec(memory_space=pl.ANY),
            pl.BlockSpec(memory_space=pltpu.SMEM),
        ],
        out_specs=pl.BlockSpec(memory_space=pltpu.VMEM),
        scratch_shapes=[
            pltpu.VMEM((nao // ROWS, 2, nao, ROWS, depth), BF16),
            pltpu.VMEM((2 * nemb, 2 * nao), BF16),
            pltpu.VMEM((2 * nemb, 2 * nao), BF16),
            pltpu.VMEM((2 * nemb, nao, depth), BF16),
            pltpu.VMEM((CORES * ZS * XS, 2, nao // YS, nemb), BF16),
            pltpu.VMEM((YS, 2, nao // YS, nemb), BF16),
            pltpu.VMEM((CHUNKS, ZS * XS) + unit, BF16),
            pltpu.VMEM((CHUNKS, ZS * XS) + unit, BF16),
            pltpu.VMEM((CHUNKS, ZS * XS) + unit, BF16),
            pltpu.VMEM((CHUNKS,) + unit, BF16),
            pltpu.VMEM((CHUNKS,) + unit, BF16),
            pltpu.VMEM((CHUNKS, XS) + unit, BF16),
            pltpu.VMEM((CHUNKS, XS) + unit, BF16),
            pltpu.VMEM((CHUNKS,) + unit, BF16),
            pltpu.VMEM((2 * YS, CHUNKS) + unit, BF16),
            pltpu.VMEM((2 * YS, 2 * nemb, 2 * depth), BF16),
            pltpu.SemaphoreType.DMA((nao // ROWS,)),
            pltpu.SemaphoreType.DMA((8,)),
            pltpu.SemaphoreType.DMA((8,)),
            pltpu.SemaphoreType.DMA((17, CHUNKS)),
            pltpu.SemaphoreType.DMA((17, CHUNKS)),
            pltpu.SemaphoreType.DMA,
        ],
        compiler_params=pltpu.CompilerParams(
            collective_id=0, has_side_effects=True, vmem_limit_bytes=66_000_000
        ),
    )(orbital_coef, tensor, shifted_index)


def solution(mesh):
    placed = (P(None, "ka", None, None), P(None, "ka", None, None, "aux"), P())
    return jax.shard_map(
        local, mesh=mesh, in_specs=placed, out_specs=P(None, "ka", "aux"), check_vma=False
    )
```

```python
import functools

import jax
import jax.numpy as jnp
from jax import lax
from jax.experimental import pallas as pl
from jax.experimental.pallas import tpu as pltpu
from jax.sharding import PartitionSpec as P

F32, BF16 = jnp.float32, jnp.bfloat16
MESH = pl.DeviceIdType.MESH
ROWS = 16
CHUNKS = 8
SLOTS = 3
PICK_AT = 8
UNROLL = 4
CORES, ZS, XS, YS = 2, 4, 2, 4
NKA = CORES * ZS * XS
KINDS = 20


def matmul(left, right):
    return lax.dot_general(left, right, (((1,), (0,)), ((), ())), preferred_element_type=F32)


def matmul_nt(left, right):
    return lax.dot_general(left, right, (((1,), (1,)), ((), ())), preferred_element_type=F32)


def kernel(coef, tensor, index, out, blocks, turned, raw, w1f, w1, w2, half, cg, cs, away, mine, other, za, zb, zm, zp, xr, ra, rb, fg, cols,
           lsem, gsend, grecv, dsend, drecv, local_sem):
    nao = coef.shape[2]
    part = nao // YS
    nblocks = nao // ROWS
    ka, aux = lax.axis_index("ka"), lax.axis_index("aux")
    core, z, x = lax.rem(ka, CORES), lax.rem(lax.div(ka, CORES), ZS), lax.div(ka, CORES * ZS)
    y, xh = lax.rem(aux, YS), lax.div(aux, YS)
    up, down, across = lax.rem(z + 1, ZS), lax.rem(z + ZS - 1, ZS), lax.rem(z + 2, ZS)
    y_up, y_down = lax.rem(y + 1, YS), lax.rem(y + YS - 1, YS)
    aux_far = lax.rem(aux + YS, 2 * YS)
    to_core = (ka + 1 - 2 * core, aux)
    to_x = (lax.rem(ka + CORES * ZS, XS * CORES * ZS), aux)
    to_up = (x * CORES * ZS + up * CORES + core, aux)
    to_down = (x * CORES * ZS + down * CORES + core, aux)
    to_y_up, to_y_down = (ka, xh * YS + y_up), (ka, xh * YS + y_down)
    to_out = (lax.rem(ka + CORES * ZS, XS * CORES * ZS), aux_far)
    x_other = 1 - x

    def load(i):
        return pltpu.make_async_copy(tensor.at[:, :, pl.ds(pl.multiple_of(i * ROWS, ROWS), ROWS), :], blocks.at[lax.rem(i, SLOTS)], lsem.at[lax.rem(i, SLOTS)])

    for i in range(SLOTS - 1):
        load(i).start()

    barrier = pltpu.get_barrier_semaphore()
    to_ka = [(lax.rem(ka + n, NKA), aux) for n in range(1, NKA)]
    to_ys = [(ka, xh * YS + lax.rem(y + n, YS)) for n in range(1, YS)]
    partners = to_ka + to_ys + [to_out]
    for partner in partners:
        pl.semaphore_signal(barrier, inc=1, device_id=partner, device_id_type=MESH)

    def send(src, dst, send_sem, recv_sem, where):
        return pltpu.make_async_remote_copy(
            src_ref=src, dst_ref=dst, send_sem=send_sem, recv_sem=recv_sem, device_id=where, device_id_type=MESH
        )

    own_rows = coef.at[:, 0, pl.ds(pl.multiple_of(y * part, 16), part), :]
    keep = pltpu.make_async_copy(own_rows, cg.at[ka], local_sem)
    spread = [send(own_rows, cg.at[ka], gsend.at[n], grecv.at[n], where) for n, where in enumerate(to_ka)]
    collect = [
        send(cs.at[y], cs.at[y], gsend.at[NKA - 1 + n], grecv.at[NKA - 1 + n], where) for n, where in enumerate(to_ys)
    ]
    keep.start()
    left_real, left_imag = coef[0, 0], coef[1, 0]
    left = jnp.concatenate(
        [jnp.concatenate([left_real, -left_imag], 1), jnp.concatenate([left_imag, left_real], 1)], 0
    ).T.astype(F32)
    for k in range(3):
        w1f[k] = left[:, k * 128 : k * 128 + 128]
    for h in range(2):
        for n in range(8):
            rows = pl.ds((n // 4) * 128 + h * 4 + n % 4, 16, stride=8)
            w1[h, n * 16 : n * 16 + 16] = jnp.concatenate([w1f[k, rows, :] for k in range(3)], 1).astype(BF16)

    def transform(h, i):
        for n in range(0, ROWS, 2):
            got = matmul(w1[h], jnp.concatenate([turned[i, n], turned[i, n + 1]], 1)).astype(BF16)
            raw[n] = got[:, :128]
            raw[n + 1] = got[:, 128:]
        at = pl.ds(pl.multiple_of(i * ROWS, ROWS), ROWS)
        for m in range(0, 128, 16):
            half[h, m : m + 16, at, :] = jnp.swapaxes(raw[:, m : m + 16, :], 0, 1)

    def first(i, carry):
        @pl.when(i == PICK_AT)
        def _():
            keep.wait()
            for copy in spread:
                copy.wait()
            cs[y] = cg[index[ka]]
            for copy in collect:
                copy.start()

        @pl.when(i + SLOTS - 1 < nblocks)
        def _():
            load(i + SLOTS - 1).start()

        load(i).wait()
        for c in range(2):
            for m in range(0, nao, 16):
                piece = blocks[lax.rem(i, SLOTS), c, m : m + 16]
                turned[i, :, c * nao + m : c * nao + m + 16, :] = jnp.swapaxes(piece, 0, 1)
        transform(0, i)
        return carry

    first(0, 0)
    pl.semaphore_wait(barrier, len(partners))
    for copy in spread:
        copy.start()
    lax.fori_loop(1, nblocks, first, 0)

    for copy in collect:
        copy.wait()
    right_real = jnp.concatenate([cs[n, 0] for n in range(YS)], 0)
    right_imag = jnp.concatenate([cs[n, 1] for n in range(YS)], 0)
    w2[...] = jnp.concatenate(
        [jnp.concatenate([right_real, right_imag], 1), jnp.concatenate([-right_imag, right_real], 1)], 0
    ).T

    def second(begin, end):
        def one(i, carry):
            transform(1, i)
            return carry

        lax.fori_loop(begin, end, one, 0)

    def pairs(cc, target, into):
        def one(q, carry):
            t = lax.rem(q, 2) * 8 + lax.div(q, 2) * 2 + target
            sides = []
            for c in (2 * cc, 2 * cc + 1):
                row = c % 4 * 16 + t
                sides.append(jnp.concatenate([half[c // 4, row], half[c // 4, 64 + row]], 0))
            got = matmul(w2[...], jnp.concatenate(sides, 1)).astype(into.dtype)
            into[2 * cc, q] = got[:, :128]
            into[2 * cc + 1, q] = got[:, 128:]
            return carry

        lax.fori_loop(0, 8, one, 0, unroll=UNROLL)

    def add(dst, srcs, scale=None):
        def one(i, carry):
            at = pl.ds(pl.multiple_of(i * 64, 64), 64)
            total = srcs[0][at]
            for src in srcs[1:]:
                total = total + src[at].astype(F32)
            if scale is not None:
                total = total * scale
            dst[at] = total.astype(BF16)
            return carry

        lax.fori_loop(0, 4, one, 0)

    def move(kind, c):
        def one(src, dst, where):
            return send(src, dst, dsend.at[kind, c], drecv.at[kind, c], where)

        if kind == 0:
            both = pl.ds(2 * c, 2)
            return one(away.at[both], other.at[both], to_core)
        if kind == 1:
            return one(other.at[c, across * 2], za.at[c], to_up)
        if kind == 2:
            return one(other.at[c, across * 2 + 1], zb.at[c], to_down)
        if kind in (3, 5):
            n = 1 if kind == 3 else 0
            return one(other.at[c, up * 2 + n], zm.at[c, n], to_up)
        if kind in (4, 6):
            n = 0 if kind == 4 else 1
            return one(other.at[c, down * 2 + n], zp.at[c, n], to_down)
        if kind == 7:
            return one(other.at[c, z * 2 + x_other], xr.at[c], to_x)
        low, high = pl.ds(0, 128), pl.ds(128, 128)
        if kind == 8:
            return one(fg.at[aux, c, low], ra.at[c], to_x)
        if kind == 17:
            return one(fg.at[aux, c, high], rb.at[c], to_out)
        if kind == 18:
            return one(ra.at[c], fg.at[aux, c, low], to_out)
        if kind == 19:
            return one(rb.at[c], fg.at[aux_far, c, high], to_x)
        if kind in (9, 10):
            return one(fg.at[aux, c], fg.at[aux, c], to_y_up if kind == 9 else to_y_down)
        if kind in (11, 12):
            return one(fg.at[aux_far, c], fg.at[aux_far, c], to_y_up if kind == 11 else to_y_down)
        base = (xh if kind < 15 else 1 - xh) * YS
        if kind in (13, 15):
            piece = fg.at[base + y_down, c, low]
            return one(piece, piece, to_y_up)
        piece = fg.at[base + y_up, c, high]
        return one(piece, piece, to_y_down)

    def pair_away(cc):
        pairs(cc, 1 - core, away)
        move(0, cc).start()

    def pair_mine(cc):
        pairs(cc, core, mine)

    def wait_core(cc):
        move(0, cc).wait_recv()

    def stage_a(c):
        for kind, q in ((1, across * 2), (2, across * 2 + 1)):
            add(other.at[c, q], (mine.at[c, q], other.at[c, q]))
            move(kind, c).start()

    def stage_a2(c):
        for kind, q in ((3, up * 2 + 1), (4, down * 2)):
            add(other.at[c, q], (mine.at[c, q], other.at[c, q]))
            move(kind, c).start()

    def stage_b(c):
        for first_kind, kind, q, got in ((1, 5, up * 2, za), (2, 6, down * 2 + 1, zb)):
            move(first_kind, c).wait_recv()
            add(other.at[c, q], (mine.at[c, q], other.at[c, q], got.at[c]))
            move(kind, c).start()

    def stage_d(c):
        for kind in (3, 4, 5, 6):
            move(kind, c).wait_recv()
        q = z * 2 + x_other
        add(other.at[c, q], (mine.at[c, q], other.at[c, q], zm.at[c, x_other], zp.at[c, x_other]))
        move(7, c).start()

    def stage_e(c):
        move(7, c).wait_recv()
        q = z * 2 + x
        add(fg.at[aux, c], (mine.at[c, q], other.at[c, q], zm.at[c, x], zp.at[c, x], xr.at[c]), 1 / (CORES * ZS * XS))
        for kind in (8, 17, 9, 10):
            move(kind, c).start()

    def stage_r(c):
        for wait_kind, kind in ((8, 18), (17, 19)):
            move(wait_kind, c).wait_recv()
            move(kind, c).start()

    def stage_g(c):
        move(18, c).wait_recv()
        move(19, c).wait_recv()
        move(11, c).start()
        move(12, c).start()

    def stage_h(c):
        for wait_kind, kind in ((9, 13), (10, 14)):
            move(wait_kind, c).wait_recv()
            move(kind, c).start()

    def stage_h2(c):
        for wait_kind, kind in ((11, 15), (12, 16)):
            move(wait_kind, c).wait_recv()
            move(kind, c).start()

    def stage_i(c):
        for kind in (13, 14, 15, 16):
            move(kind, c).wait_recv()

    pair_away(0)
    pair_mine(0)
    second(0, 1)
    pair_away(1)
    pair_mine(1)
    wait_core(0)
    stage_a(0)
    stage_a(1)
    second(1, 3)
    stage_a2(0)
    second(3, 4)
    wait_core(1)
    second(4, 5)
    stage_a2(1)
    second(5, 6)
    stage_b(0)
    second(6, 8)
    stage_b(1)
    second(8, 12)
    stage_a(2)
    pair_away(2)
    stage_a2(2)
    pair_away(3)
    stage_d(0)
    pair_mine(2)
    stage_a(3)
    stage_d(1)
    pair_mine(3)
    wait_core(2)
    stage_a(4)
    stage_b(2)
    stage_e(0)
    wait_core(3)
    stage_a2(4)
    stage_e(1)
    stage_r(0)
    stage_a2(3)
    stage_b(3)
    stage_b(4)
    stage_h(0)
    stage_r(1)
    stage_d(2)
    stage_h(1)
    stage_g(0)
    stage_g(1)
    stage_a(5)
    stage_e(2)
    stage_a2(5)
    stage_h2(0)
    stage_d(3)
    stage_a(6)
    stage_h2(1)
    stage_d(4)
    stage_r(2)
    stage_a2(6)
    stage_h(2)
    stage_b(5)
    stage_e(3)
    stage_e(4)
    stage_a(7)
    stage_g(2)
    stage_b(6)
    stage_r(3)
    stage_h(3)
    stage_r(4)
    stage_a2(7)
    stage_h(4)
    stage_d(5)
    stage_g(3)
    stage_h2(2)
    stage_g(4)
    stage_b(7)
    stage_d(6)
    stage_e(5)
    stage_h2(3)
    stage_d(7)
    stage_h2(4)
    stage_e(6)
    stage_r(5)
    stage_h(5)
    stage_e(7)
    stage_r(6)
    stage_h(6)
    stage_g(5)
    stage_r(7)
    stage_g(6)
    stage_h(7)
    stage_g(7)
    stage_h2(5)
    stage_h2(6)
    stage_h2(7)
    for c in range(CHUNKS):
        stage_i(c)

    for j in range(2 * YS):
        column = fg[j, aux]
        real, imag = column[:128], column[128:]
        cols[j] = jnp.concatenate(
            [jnp.concatenate([real, imag], 1), jnp.concatenate([-imag, real], 1)], 0
        )

    def tile(i, carry):
        total = jnp.zeros((256, 256), F32)
        for j in range(2 * YS):
            rows = jnp.concatenate(
                [jnp.concatenate([fg[j, 2 * i + n, :128], fg[j, 2 * i + n, 128:]], 1) for n in range(2)], 0
            )
            total = total + matmul_nt(rows, cols[j])
        at = pl.ds(pl.multiple_of(i * 256, 256), 256)
        out[0, at, :] = total[:, :128]
        out[1, at, :] = total[:, 128:]
        return carry

    lax.fori_loop(0, CHUNKS // 2, tile, 0)

    for kind in range(KINDS):
        for c in range(CHUNKS if kind else CHUNKS // 2):
            move(kind, c).wait_send()


def local(orbital_coef, dftensor, shifted_index):
    nao, nemb = orbital_coef.shape[2:]
    depth = dftensor.shape[-1]
    tensor = dftensor.reshape(2, nao, nao, depth)
    unit = (2 * nemb, depth)
    return pl.pallas_call(
        kernel,
        out_shape=jax.ShapeDtypeStruct((2, 8 * nemb, nemb), F32),
        in_specs=[
            pl.BlockSpec(memory_space=pltpu.VMEM),
            pl.BlockSpec(memory_space=pl.ANY),
            pl.BlockSpec(memory_space=pltpu.SMEM),
        ],
        out_specs=pl.BlockSpec(memory_space=pltpu.VMEM),
        scratch_shapes=[
            pltpu.VMEM((SLOTS, 2, nao, ROWS, depth), BF16),
            pltpu.VMEM((nao // ROWS, ROWS, 2 * nao, depth), BF16),
            pltpu.VMEM((ROWS, nemb, depth), BF16),
            pltpu.VMEM((3, 2 * nemb, 128), F32),
            pltpu.VMEM((2, nemb, 2 * nao), BF16),
            pltpu.VMEM((2 * nemb, 2 * nao), BF16),
            pltpu.VMEM((2, nemb, nao, depth), BF16),
            pltpu.VMEM((CORES * ZS * XS, 2, nao // YS, nemb), BF16),
            pltpu.VMEM((YS, 2, nao // YS, nemb), BF16),
            pltpu.VMEM((CHUNKS, ZS * XS) + unit, BF16),
            pltpu.VMEM((CHUNKS, ZS * XS) + unit, F32),
            pltpu.VMEM((CHUNKS, ZS * XS) + unit, BF16),
            pltpu.VMEM((CHUNKS,) + unit, BF16),
            pltpu.VMEM((CHUNKS,) + unit, BF16),
            pltpu.VMEM((CHUNKS, XS) + unit, BF16),
            pltpu.VMEM((CHUNKS, XS) + unit, BF16),
            pltpu.VMEM((CHUNKS,) + unit, BF16),
            pltpu.VMEM((CHUNKS, nemb, depth), BF16),
            pltpu.VMEM((CHUNKS, nemb, depth), BF16),
            pltpu.VMEM((2 * YS, CHUNKS) + unit, BF16),
            pltpu.VMEM((2 * YS, 2 * nemb, 2 * depth), BF16),
            pltpu.SemaphoreType.DMA((SLOTS,)),
            pltpu.SemaphoreType.DMA((NKA + YS - 2,)),
            pltpu.SemaphoreType.DMA((NKA + YS - 2,)),
            pltpu.SemaphoreType.DMA((KINDS, CHUNKS)),
            pltpu.SemaphoreType.DMA((KINDS, CHUNKS)),
            pltpu.SemaphoreType.DMA,
        ],
        compiler_params=pltpu.CompilerParams(
            collective_id=0, has_side_effects=True, vmem_limit_bytes=67_000_000
        ),
    )(orbital_coef, tensor, shifted_index)


def solution(mesh):
    placed = (P(None, "ka", None, None), P(None, "ka", None, None, "aux"), P())
    return jax.shard_map(
        local, mesh=mesh, in_specs=placed, out_specs=P(None, "ka", "aux"), check_vma=False
    )
```

```python
import functools

import jax
import jax.numpy as jnp
from jax import lax
from jax.experimental import pallas as pl
from jax.experimental.pallas import tpu as pltpu
from jax.sharding import PartitionSpec as P

F32, BF16 = jnp.float32, jnp.bfloat16
MESH = pl.DeviceIdType.MESH
ROWS = 16
CHUNKS = 8
SLOTS = 3
PICK_AT = 9
UNROLL = 4
CORES, ZS, XS, YS = 2, 4, 2, 4
NKA = CORES * ZS * XS
KINDS = 17


def matmul(left, right):
    return lax.dot_general(left, right, (((1,), (0,)), ((), ())), preferred_element_type=F32)


def matmul_nt(left, right):
    return lax.dot_general(left, right, (((1,), (1,)), ((), ())), preferred_element_type=F32)


def kernel(coef, tensor, index, out, blocks, turned, raw, w1f, w1, w2, half, cg, cs, away, mine, other, za, zb, zm, zp, xr, fg, cols,
           lsem, gsend, grecv, dsend, drecv, local_sem):
    nao = coef.shape[2]
    part = nao // YS
    nblocks = nao // ROWS
    ka, aux = lax.axis_index("ka"), lax.axis_index("aux")
    core, z, x = lax.rem(ka, CORES), lax.rem(lax.div(ka, CORES), ZS), lax.div(ka, CORES * ZS)
    y, xh = lax.rem(aux, YS), lax.div(aux, YS)
    up, down, across = lax.rem(z + 1, ZS), lax.rem(z + ZS - 1, ZS), lax.rem(z + 2, ZS)
    y_up, y_down = lax.rem(y + 1, YS), lax.rem(y + YS - 1, YS)
    aux_far = lax.rem(aux + YS, 2 * YS)
    to_core = (ka + 1 - 2 * core, aux)
    to_x = (lax.rem(ka + CORES * ZS, XS * CORES * ZS), aux)
    to_up = (x * CORES * ZS + up * CORES + core, aux)
    to_down = (x * CORES * ZS + down * CORES + core, aux)
    to_y_up, to_y_down = (ka, xh * YS + y_up), (ka, xh * YS + y_down)
    to_far = (ka, aux_far)
    x_other = 1 - x

    def load(i):
        return pltpu.make_async_copy(tensor.at[:, :, pl.ds(pl.multiple_of(i * ROWS, ROWS), ROWS), :], blocks.at[lax.rem(i, SLOTS)], lsem.at[lax.rem(i, SLOTS)])

    for i in range(SLOTS - 1):
        load(i).start()

    barrier = pltpu.get_barrier_semaphore()
    to_ka = [(lax.rem(ka + n, NKA), aux) for n in range(1, NKA)]
    to_ys = [(ka, xh * YS + lax.rem(y + n, YS)) for n in range(1, YS)]
    partners = to_ka + to_ys + [to_far]
    for partner in partners:
        pl.semaphore_signal(barrier, inc=1, device_id=partner, device_id_type=MESH)

    def send(src, dst, send_sem, recv_sem, where):
        return pltpu.make_async_remote_copy(
            src_ref=src, dst_ref=dst, send_sem=send_sem, recv_sem=recv_sem, device_id=where, device_id_type=MESH
        )

    own_rows = coef.at[:, 0, pl.ds(pl.multiple_of(y * part, 16), part), :]
    keep = pltpu.make_async_copy(own_rows, cg.at[ka], local_sem)
    spread = [send(own_rows, cg.at[ka], gsend.at[n], grecv.at[n], where) for n, where in enumerate(to_ka)]
    collect = [
        send(cs.at[y], cs.at[y], gsend.at[NKA - 1 + n], grecv.at[NKA - 1 + n], where) for n, where in enumerate(to_ys)
    ]
    keep.start()
    left_real, left_imag = coef[0, 0], coef[1, 0]
    left = jnp.concatenate(
        [jnp.concatenate([left_real, -left_imag], 1), jnp.concatenate([left_imag, left_real], 1)], 0
    ).T.astype(F32)
    for k in range(3):
        w1f[k] = left[:, k * 128 : k * 128 + 128]
    for h in range(2):
        for n in range(8):
            rows = pl.ds((n // 4) * 128 + h * 4 + n % 4, 16, stride=8)
            w1[h, n * 16 : n * 16 + 16] = jnp.concatenate([w1f[k, rows, :] for k in range(3)], 1).astype(BF16)

    def transform(h, i):
        for n in range(0, ROWS, 2):
            got = matmul(w1[h], jnp.concatenate([turned[i, n], turned[i, n + 1]], 1)).astype(BF16)
            raw[n] = got[:, :128]
            raw[n + 1] = got[:, 128:]
        at = pl.ds(pl.multiple_of(i * ROWS, ROWS), ROWS)
        for m in range(0, 128, 16):
            half[h, m : m + 16, at, :] = jnp.swapaxes(raw[:, m : m + 16, :], 0, 1)

    def first(i, carry):
        @pl.when(i == PICK_AT)
        def _():
            keep.wait()
            for copy in spread:
                copy.wait()
            cs[y] = cg[index[ka]]
            for copy in collect:
                copy.start()

        @pl.when(i + SLOTS - 1 < nblocks)
        def _():
            load(i + SLOTS - 1).start()

        load(i).wait()
        for c in range(2):
            for m in range(0, nao, 16):
                piece = blocks[lax.rem(i, SLOTS), c, m : m + 16]
                turned[i, :, c * nao + m : c * nao + m + 16, :] = jnp.swapaxes(piece, 0, 1)
        transform(0, i)
        return carry

    first(0, 0)
    pl.semaphore_wait(barrier, len(partners))
    for copy in spread:
        copy.start()
    lax.fori_loop(1, nblocks, first, 0)

    for copy in collect:
        copy.wait()
    right_real = jnp.concatenate([cs[n, 0] for n in range(YS)], 0)
    right_imag = jnp.concatenate([cs[n, 1] for n in range(YS)], 0)
    w2[...] = jnp.concatenate(
        [jnp.concatenate([right_real, right_imag], 1), jnp.concatenate([-right_imag, right_real], 1)], 0
    ).T

    def second(begin, end):
        def one(i, carry):
            transform(1, i)
            return carry

        lax.fori_loop(begin, end, one, 0)

    def pairs(cc, target, into):
        def one(q, carry):
            t = lax.rem(q, 2) * 8 + lax.div(q, 2) * 2 + target
            sides = []
            for c in (2 * cc, 2 * cc + 1):
                row = c % 4 * 16 + t
                sides.append(jnp.concatenate([half[c // 4, row], half[c // 4, 64 + row]], 0))
            got = matmul(w2[...], jnp.concatenate(sides, 1)).astype(into.dtype)
            into[2 * cc, q] = got[:, :128]
            into[2 * cc + 1, q] = got[:, 128:]
            return carry

        lax.fori_loop(0, 8, one, 0, unroll=UNROLL)

    def add(dst, srcs, scale=None):
        def one(i, carry):
            at = pl.ds(pl.multiple_of(i * 64, 64), 64)
            total = srcs[0][at]
            for src in srcs[1:]:
                total = total + src[at].astype(F32)
            if scale is not None:
                total = total * scale
            dst[at] = total.astype(BF16)
            return carry

        lax.fori_loop(0, 4, one, 0)

    def move(kind, c):
        def one(src, dst, where):
            return send(src, dst, dsend.at[kind, c], drecv.at[kind, c], where)

        if kind == 0:
            both = pl.ds(2 * c, 2)
            return one(away.at[both], other.at[both], to_core)
        if kind == 1:
            return one(other.at[c, across * 2], za.at[c], to_up)
        if kind == 2:
            return one(other.at[c, across * 2 + 1], zb.at[c], to_down)
        if kind in (3, 5):
            n = 1 if kind == 3 else 0
            return one(other.at[c, up * 2 + n], zm.at[c, n], to_up)
        if kind in (4, 6):
            n = 0 if kind == 4 else 1
            return one(other.at[c, down * 2 + n], zp.at[c, n], to_down)
        if kind == 7:
            return one(other.at[c, z * 2 + x_other], xr.at[c], to_x)
        low, high = pl.ds(0, 128), pl.ds(128, 128)
        if kind == 8:
            return one(fg.at[aux, c], fg.at[aux, c], to_far)
        if kind in (9, 10):
            return one(fg.at[aux, c], fg.at[aux, c], to_y_up if kind == 9 else to_y_down)
        if kind in (11, 12):
            return one(fg.at[aux_far, c], fg.at[aux_far, c], to_y_up if kind == 11 else to_y_down)
        base = (xh if kind < 15 else 1 - xh) * YS
        if kind in (13, 15):
            piece = fg.at[base + y_down, c, low]
            return one(piece, piece, to_y_up)
        piece = fg.at[base + y_up, c, high]
        return one(piece, piece, to_y_down)

    def pair_away(cc):
        pairs(cc, 1 - core, away)
        move(0, cc).start()

    def pair_mine(cc):
        pairs(cc, core, mine)

    def wait_core(cc):
        move(0, cc).wait_recv()

    def stage_a(c):
        for kind, q in ((1, across * 2), (2, across * 2 + 1)):
            add(other.at[c, q], (mine.at[c, q], other.at[c, q]))
            move(kind, c).start()

    def stage_a2(c):
        for kind, q in ((3, up * 2 + 1), (4, down * 2)):
            add(other.at[c, q], (mine.at[c, q], other.at[c, q]))
            move(kind, c).start()

    def stage_b(c):
        for first_kind, kind, q, got in ((1, 5, up * 2, za), (2, 6, down * 2 + 1, zb)):
            move(first_kind, c).wait_recv()
            add(other.at[c, q], (mine.at[c, q], other.at[c, q], got.at[c]))
            move(kind, c).start()

    def stage_d(c):
        for kind in (3, 4, 5, 6):
            move(kind, c).wait_recv()
        q = z * 2 + x_other
        add(other.at[c, q], (mine.at[c, q], other.at[c, q], zm.at[c, x_other], zp.at[c, x_other]))
        move(7, c).start()

    def stage_e(c):
        move(7, c).wait_recv()
        q = z * 2 + x
        add(fg.at[aux, c], (mine.at[c, q], other.at[c, q], zm.at[c, x], zp.at[c, x], xr.at[c]), 1 / (CORES * ZS * XS))
        for kind in (8, 9, 10):
            move(kind, c).start()

    def stage_g(c):
        move(8, c).wait_recv()
        move(11, c).start()
        move(12, c).start()

    def stage_h(c):
        for wait_kind, kind in ((9, 13), (10, 14)):
            move(wait_kind, c).wait_recv()
            move(kind, c).start()

    def stage_h2(c):
        for wait_kind, kind in ((11, 15), (12, 16)):
            move(wait_kind, c).wait_recv()
            move(kind, c).start()

    def stage_i(c):
        for kind in (13, 14, 15, 16):
            move(kind, c).wait_recv()

    pair_away(0)
    pair_mine(0)
    second(0, 1)
    pair_away(1)
    second(1, 2)
    pair_mine(1)
    wait_core(0)
    stage_a(0)
    stage_a2(0)
    second(2, 4)
    stage_a(1)
    second(4, 5)
    wait_core(1)
    second(5, 6)
    stage_a(2)
    second(6, 7)
    stage_b(0)
    second(7, 10)
    stage_a2(1)
    second(10, 12)
    stage_b(1)
    pair_away(2)
    pair_mine(2)
    stage_a2(2)
    stage_b(2)
    pair_away(3)
    stage_d(0)
    pair_mine(3)
    wait_core(2)
    stage_a(3)
    stage_d(1)
    stage_a(4)
    wait_core(3)
    stage_e(0)
    stage_a2(3)
    stage_d(2)
    stage_a2(4)
    stage_e(1)
    stage_b(3)
    stage_h(0)
    stage_b(4)
    stage_e(2)
    stage_h(1)
    stage_a(5)
    stage_g(0)
    stage_a2(5)
    stage_d(3)
    stage_g(1)
    stage_h(2)
    stage_a(6)
    stage_d(4)
    stage_a2(6)
    stage_g(2)
    stage_h2(0)
    stage_b(5)
    stage_e(3)
    stage_h2(1)
    stage_a(7)
    stage_e(4)
    stage_b(6)
    stage_h2(2)
    stage_a2(7)
    stage_h(3)
    stage_d(5)
    stage_g(3)
    stage_b(7)
    stage_h(4)
    stage_g(4)
    stage_d(6)
    stage_e(5)
    stage_h2(3)
    stage_d(7)
    stage_e(6)
    stage_h2(4)
    stage_h(5)
    stage_e(7)
    stage_h(6)
    stage_g(5)
    stage_g(6)
    stage_h(7)
    stage_g(7)
    stage_h2(5)
    stage_h2(6)
    stage_h2(7)
    for c in range(CHUNKS):
        stage_i(c)

    for j in range(2 * YS):
        column = fg[j, aux]
        real, imag = column[:128], column[128:]
        cols[j] = jnp.concatenate(
            [jnp.concatenate([real, imag], 1), jnp.concatenate([-imag, real], 1)], 0
        )

    def tile(i, carry):
        total = jnp.zeros((256, 256), F32)
        for j in range(2 * YS):
            rows = jnp.concatenate(
                [jnp.concatenate([fg[j, 2 * i + n, :128], fg[j, 2 * i + n, 128:]], 1) for n in range(2)], 0
            )
            total = total + matmul_nt(rows, cols[j])
        at = pl.ds(pl.multiple_of(i * 256, 256), 256)
        out[0, at, :] = total[:, :128]
        out[1, at, :] = total[:, 128:]
        return carry

    lax.fori_loop(0, CHUNKS // 2, tile, 0)

    for kind in range(KINDS):
        for c in range(CHUNKS if kind else CHUNKS // 2):
            move(kind, c).wait_send()


def local(orbital_coef, dftensor, shifted_index):
    nao, nemb = orbital_coef.shape[2:]
    depth = dftensor.shape[-1]
    tensor = dftensor.reshape(2, nao, nao, depth)
    unit = (2 * nemb, depth)
    return pl.pallas_call(
        kernel,
        out_shape=jax.ShapeDtypeStruct((2, 8 * nemb, nemb), F32),
        in_specs=[
            pl.BlockSpec(memory_space=pltpu.VMEM),
            pl.BlockSpec(memory_space=pl.ANY),
            pl.BlockSpec(memory_space=pltpu.SMEM),
        ],
        out_specs=pl.BlockSpec(memory_space=pltpu.VMEM),
        scratch_shapes=[
            pltpu.VMEM((SLOTS, 2, nao, ROWS, depth), BF16),
            pltpu.VMEM((nao // ROWS, ROWS, 2 * nao, depth), BF16),
            pltpu.VMEM((ROWS, nemb, depth), BF16),
            pltpu.VMEM((3, 2 * nemb, 128), F32),
            pltpu.VMEM((2, nemb, 2 * nao), BF16),
            pltpu.VMEM((2 * nemb, 2 * nao), BF16),
            pltpu.VMEM((2, nemb, nao, depth), BF16),
            pltpu.VMEM((CORES * ZS * XS, 2, nao // YS, nemb), BF16),
            pltpu.VMEM((YS, 2, nao // YS, nemb), BF16),
            pltpu.VMEM((CHUNKS, ZS * XS) + unit, BF16),
            pltpu.VMEM((CHUNKS, ZS * XS) + unit, F32),
            pltpu.VMEM((CHUNKS, ZS * XS) + unit, BF16),
            pltpu.VMEM((CHUNKS,) + unit, BF16),
            pltpu.VMEM((CHUNKS,) + unit, BF16),
            pltpu.VMEM((CHUNKS, XS) + unit, BF16),
            pltpu.VMEM((CHUNKS, XS) + unit, BF16),
            pltpu.VMEM((CHUNKS,) + unit, BF16),
            pltpu.VMEM((2 * YS, CHUNKS) + unit, BF16),
            pltpu.VMEM((2 * YS, 2 * nemb, 2 * depth), BF16),
            pltpu.SemaphoreType.DMA((SLOTS,)),
            pltpu.SemaphoreType.DMA((NKA + YS - 2,)),
            pltpu.SemaphoreType.DMA((NKA + YS - 2,)),
            pltpu.SemaphoreType.DMA((KINDS, CHUNKS)),
            pltpu.SemaphoreType.DMA((KINDS, CHUNKS)),
            pltpu.SemaphoreType.DMA,
        ],
        compiler_params=pltpu.CompilerParams(
            collective_id=0, has_side_effects=True, vmem_limit_bytes=67_000_000
        ),
    )(orbital_coef, tensor, shifted_index)


def solution(mesh):
    placed = (P(None, "ka", None, None), P(None, "ka", None, None, "aux"), P())
    return jax.shard_map(
        local, mesh=mesh, in_specs=placed, out_specs=P(None, "ka", "aux"), check_vma=False
    )
```

```python
import functools

import jax
import jax.numpy as jnp
from jax import lax
from jax.experimental import pallas as pl
from jax.experimental.pallas import tpu as pltpu
from jax.sharding import PartitionSpec as P

F32, BF16 = jnp.float32, jnp.bfloat16
MESH = pl.DeviceIdType.MESH
ROWS = 16
CHUNKS = 8
SLOTS = 3
PICK_AT = 9
UNROLL = 8
CORES, ZS, XS, YS = 2, 4, 2, 4
NKA = CORES * ZS * XS
KINDS = 17


def matmul(left, right):
    return lax.dot_general(left, right, (((1,), (0,)), ((), ())), preferred_element_type=F32)


def matmul_nt(left, right):
    return lax.dot_general(left, right, (((1,), (1,)), ((), ())), preferred_element_type=F32)


def kernel(coef, tensor, index, out, blocks, turned, raw, w1f, w1, w2, half, cg, cs, away, mine, other, za, zb, zm, zp, xr, fg, cols,
           lsem, gsend, grecv, dsend, drecv, local_sem):
    nao = coef.shape[2]
    part = nao // YS
    nblocks = nao // ROWS
    ka, aux = lax.axis_index("ka"), lax.axis_index("aux")
    core, z, x = lax.rem(ka, CORES), lax.rem(lax.div(ka, CORES), ZS), lax.div(ka, CORES * ZS)
    y, xh = lax.rem(aux, YS), lax.div(aux, YS)
    up, down, across = lax.rem(z + 1, ZS), lax.rem(z + ZS - 1, ZS), lax.rem(z + 2, ZS)
    y_up, y_down = lax.rem(y + 1, YS), lax.rem(y + YS - 1, YS)
    aux_far = lax.rem(aux + YS, 2 * YS)
    to_core = (ka + 1 - 2 * core, aux)
    to_x = (lax.rem(ka + CORES * ZS, XS * CORES * ZS), aux)
    to_up = (x * CORES * ZS + up * CORES + core, aux)
    to_down = (x * CORES * ZS + down * CORES + core, aux)
    to_y_up, to_y_down = (ka, xh * YS + y_up), (ka, xh * YS + y_down)
    to_far = (ka, aux_far)
    x_other = 1 - x

    def load(i):
        return pltpu.make_async_copy(tensor.at[:, :, pl.ds(pl.multiple_of(i * ROWS, ROWS), ROWS), :], blocks.at[lax.rem(i, SLOTS)], lsem.at[lax.rem(i, SLOTS)])

    for i in range(SLOTS - 1):
        load(i).start()

    barrier = pltpu.get_barrier_semaphore()
    to_ka = [(lax.rem(ka + n, NKA), aux) for n in range(1, NKA)]
    to_ys = [(ka, xh * YS + lax.rem(y + n, YS)) for n in range(1, YS)]
    partners = to_ka + to_ys + [to_far]
    for partner in partners:
        pl.semaphore_signal(barrier, inc=1, device_id=partner, device_id_type=MESH)

    def send(src, dst, send_sem, recv_sem, where):
        return pltpu.make_async_remote_copy(
            src_ref=src, dst_ref=dst, send_sem=send_sem, recv_sem=recv_sem, device_id=where, device_id_type=MESH
        )

    own_rows = coef.at[:, 0, pl.ds(pl.multiple_of(y * part, 16), part), :]
    keep = pltpu.make_async_copy(own_rows, cg.at[ka], local_sem)
    spread = [send(own_rows, cg.at[ka], gsend.at[n], grecv.at[n], where) for n, where in enumerate(to_ka)]
    collect = [
        send(cs.at[y], cs.at[y], gsend.at[NKA - 1 + n], grecv.at[NKA - 1 + n], where) for n, where in enumerate(to_ys)
    ]
    keep.start()
    left_real, left_imag = coef[0, 0], coef[1, 0]
    left = jnp.concatenate(
        [jnp.concatenate([left_real, -left_imag], 1), jnp.concatenate([left_imag, left_real], 1)], 0
    ).T.astype(F32)
    for k in range(3):
        w1f[k] = left[:, k * 128 : k * 128 + 128]
    for h in range(2):
        for n in range(8):
            rows = pl.ds((n // 4) * 128 + h * 4 + n % 4, 16, stride=8)
            w1[h, n * 16 : n * 16 + 16] = jnp.concatenate([w1f[k, rows, :] for k in range(3)], 1).astype(BF16)

    def transform(h, i):
        for n in range(0, ROWS, 2):
            got = matmul(w1[h], jnp.concatenate([turned[i, n], turned[i, n + 1]], 1)).astype(BF16)
            raw[n] = got[:, :128]
            raw[n + 1] = got[:, 128:]
        at = pl.ds(pl.multiple_of(i * ROWS, ROWS), ROWS)
        for m in range(0, 128, 16):
            half[h, m : m + 16, at, :] = jnp.swapaxes(raw[:, m : m + 16, :], 0, 1)

    def first(i, carry):
        @pl.when(i == PICK_AT)
        def _():
            keep.wait()
            for copy in spread:
                copy.wait()
            cs[y] = cg[index[ka]]
            for copy in collect:
                copy.start()

        @pl.when(i + SLOTS - 1 < nblocks)
        def _():
            load(i + SLOTS - 1).start()

        load(i).wait()
        for c in range(2):
            for m in range(0, nao, 16):
                piece = blocks[lax.rem(i, SLOTS), c, m : m + 16]
                turned[i, :, c * nao + m : c * nao + m + 16, :] = jnp.swapaxes(piece, 0, 1)
        transform(0, i)
        return carry

    first(0, 0)
    pl.semaphore_wait(barrier, len(partners))
    for copy in spread:
        copy.start()
    lax.fori_loop(1, nblocks, first, 0)

    for copy in collect:
        copy.wait()
    right_real = jnp.concatenate([cs[n, 0] for n in range(YS)], 0)
    right_imag = jnp.concatenate([cs[n, 1] for n in range(YS)], 0)
    w2[...] = jnp.concatenate(
        [jnp.concatenate([right_real, right_imag], 1), jnp.concatenate([-right_imag, right_real], 1)], 0
    ).T

    def second(begin, end):
        def one(i, carry):
            transform(1, i)
            return carry

        lax.fori_loop(begin, end, one, 0)

    def pairs(cc, target, into):
        def one(q, carry):
            t = lax.rem(q, 2) * 8 + lax.div(q, 2) * 2 + target
            sides = []
            for c in (2 * cc, 2 * cc + 1):
                row = c % 4 * 16 + t
                sides.append(jnp.concatenate([half[c // 4, row], half[c // 4, 64 + row]], 0))
            got = matmul(w2[...], jnp.concatenate(sides, 1)).astype(into.dtype)
            into[2 * cc, q] = got[:, :128]
            into[2 * cc + 1, q] = got[:, 128:]
            return carry

        lax.fori_loop(0, 8, one, 0, unroll=UNROLL)

    def add(dst, srcs, scale=None):
        def one(i, carry):
            at = pl.ds(pl.multiple_of(i * 64, 64), 64)
            total = srcs[0][at]
            for src in srcs[1:]:
                total = total + src[at].astype(F32)
            if scale is not None:
                total = total * scale
            dst[at] = total.astype(BF16)
            return carry

        lax.fori_loop(0, 4, one, 0)

    def move(kind, c):
        def one(src, dst, where):
            return send(src, dst, dsend.at[kind, c], drecv.at[kind, c], where)

        if kind == 0:
            both = pl.ds(2 * c, 2)
            return one(away.at[both], other.at[both], to_core)
        if kind == 1:
            return one(other.at[c, across * 2], za.at[c], to_up)
        if kind == 2:
            return one(other.at[c, across * 2 + 1], zb.at[c], to_down)
        if kind in (3, 5):
            n = 1 if kind == 3 else 0
            return one(other.at[c, up * 2 + n], zm.at[c, n], to_up)
        if kind in (4, 6):
            n = 0 if kind == 4 else 1
            return one(other.at[c, down * 2 + n], zp.at[c, n], to_down)
        if kind == 7:
            return one(other.at[c, z * 2 + x_other], xr.at[c], to_x)
        low, high = pl.ds(0, 128), pl.ds(128, 128)
        if kind == 8:
            return one(fg.at[aux, c], fg.at[aux, c], to_far)
        if kind in (9, 10):
            return one(fg.at[aux, c], fg.at[aux, c], to_y_up if kind == 9 else to_y_down)
        if kind in (11, 12):
            return one(fg.at[aux_far, c], fg.at[aux_far, c], to_y_up if kind == 11 else to_y_down)
        base = (xh if kind < 15 else 1 - xh) * YS
        if kind in (13, 15):
            piece = fg.at[base + y_down, c, low]
            return one(piece, piece, to_y_up)
        piece = fg.at[base + y_up, c, high]
        return one(piece, piece, to_y_down)

    def pair_away(cc):
        pairs(cc, 1 - core, away)
        move(0, cc).start()

    def pair_mine(cc):
        pairs(cc, core, mine)

    def wait_core(cc):
        move(0, cc).wait_recv()

    def stage_a(c):
        for kind, q in ((1, across * 2), (2, across * 2 + 1)):
            add(other.at[c, q], (mine.at[c, q], other.at[c, q]))
            move(kind, c).start()

    def stage_a2(c):
        for kind, q in ((3, up * 2 + 1), (4, down * 2)):
            add(other.at[c, q], (mine.at[c, q], other.at[c, q]))
            move(kind, c).start()

    def stage_b(c):
        for first_kind, kind, q, got in ((1, 5, up * 2, za), (2, 6, down * 2 + 1, zb)):
            move(first_kind, c).wait_recv()
            add(other.at[c, q], (mine.at[c, q], other.at[c, q], got.at[c]))
            move(kind, c).start()

    def stage_d(c):
        for kind in (3, 4, 5, 6):
            move(kind, c).wait_recv()
        q = z * 2 + x_other
        add(other.at[c, q], (mine.at[c, q], other.at[c, q], zm.at[c, x_other], zp.at[c, x_other]))
        move(7, c).start()

    def stage_e(c):
        move(7, c).wait_recv()
        q = z * 2 + x
        add(fg.at[aux, c], (mine.at[c, q], other.at[c, q], zm.at[c, x], zp.at[c, x], xr.at[c]), 1 / (CORES * ZS * XS))
        for kind in (8, 9, 10):
            move(kind, c).start()

    def stage_g(c):
        move(8, c).wait_recv()
        move(11, c).start()
        move(12, c).start()

    def stage_h(c):
        for wait_kind, kind in ((9, 13), (10, 14)):
            move(wait_kind, c).wait_recv()
            move(kind, c).start()

    def stage_h2(c):
        for wait_kind, kind in ((11, 15), (12, 16)):
            move(wait_kind, c).wait_recv()
            move(kind, c).start()

    def stage_i(c):
        for kind in (13, 14, 15, 16):
            move(kind, c).wait_recv()

    pair_away(0)
    pair_mine(0)
    second(0, 1)
    pair_away(1)
    second(1, 2)
    pair_mine(1)
    wait_core(0)
    stage_a(0)
    stage_a2(0)
    second(2, 4)
    stage_a(1)
    second(4, 5)
    wait_core(1)
    second(5, 6)
    stage_a(2)
    second(6, 7)
    stage_b(0)
    second(7, 10)
    stage_a2(1)
    second(10, 12)
    stage_b(1)
    pair_away(2)
    pair_mine(2)
    stage_a2(2)
    stage_b(2)
    pair_away(3)
    stage_d(0)
    pair_mine(3)
    wait_core(2)
    stage_a(3)
    stage_d(1)
    stage_a(4)
    wait_core(3)
    stage_e(0)
    stage_a2(3)
    stage_d(2)
    stage_a2(4)
    stage_e(1)
    stage_b(3)
    stage_h(0)
    stage_b(4)
    stage_e(2)
    stage_h(1)
    stage_a(5)
    stage_g(0)
    stage_a2(5)
    stage_d(3)
    stage_g(1)
    stage_h(2)
    stage_a(6)
    stage_d(4)
    stage_a2(6)
    stage_g(2)
    stage_h2(0)
    stage_b(5)
    stage_e(3)
    stage_h2(1)
    stage_a(7)
    stage_e(4)
    stage_b(6)
    stage_h2(2)
    stage_a2(7)
    stage_h(3)
    stage_d(5)
    stage_g(3)
    stage_b(7)
    stage_h(4)
    stage_g(4)
    stage_d(6)
    stage_e(5)
    stage_h2(3)
    stage_d(7)
    stage_e(6)
    stage_h2(4)
    stage_h(5)
    stage_e(7)
    stage_h(6)
    stage_g(5)
    stage_g(6)
    stage_h(7)
    stage_g(7)
    stage_h2(5)
    stage_h2(6)
    stage_h2(7)
    for c in range(CHUNKS):
        stage_i(c)

    for j in range(2 * YS):
        column = fg[j, aux]
        real, imag = column[:128], column[128:]
        cols[j] = jnp.concatenate(
            [jnp.concatenate([real, imag], 1), jnp.concatenate([-imag, real], 1)], 0
        )

    def tile(i, carry):
        total = jnp.zeros((256, 256), F32)
        for j in range(2 * YS):
            rows = jnp.concatenate(
                [jnp.concatenate([fg[j, 2 * i + n, :128], fg[j, 2 * i + n, 128:]], 1) for n in range(2)], 0
            )
            total = total + matmul_nt(rows, cols[j])
        at = pl.ds(pl.multiple_of(i * 256, 256), 256)
        out[0, at, :] = total[:, :128]
        out[1, at, :] = total[:, 128:]
        return carry

    lax.fori_loop(0, CHUNKS // 2, tile, 0)

    for kind in range(KINDS):
        for c in range(CHUNKS if kind else CHUNKS // 2):
            move(kind, c).wait_send()


def local(orbital_coef, dftensor, shifted_index):
    nao, nemb = orbital_coef.shape[2:]
    depth = dftensor.shape[-1]
    tensor = dftensor.reshape(2, nao, nao, depth)
    unit = (2 * nemb, depth)
    return pl.pallas_call(
        kernel,
        out_shape=jax.ShapeDtypeStruct((2, 8 * nemb, nemb), F32),
        in_specs=[
            pl.BlockSpec(memory_space=pltpu.VMEM),
            pl.BlockSpec(memory_space=pl.ANY),
            pl.BlockSpec(memory_space=pltpu.SMEM),
        ],
        out_specs=pl.BlockSpec(memory_space=pltpu.VMEM),
        scratch_shapes=[
            pltpu.VMEM((SLOTS, 2, nao, ROWS, depth), BF16),
            pltpu.VMEM((nao // ROWS, ROWS, 2 * nao, depth), BF16),
            pltpu.VMEM((ROWS, nemb, depth), BF16),
            pltpu.VMEM((3, 2 * nemb, 128), F32),
            pltpu.VMEM((2, nemb, 2 * nao), BF16),
            pltpu.VMEM((2 * nemb, 2 * nao), BF16),
            pltpu.VMEM((2, nemb, nao, depth), BF16),
            pltpu.VMEM((CORES * ZS * XS, 2, nao // YS, nemb), BF16),
            pltpu.VMEM((YS, 2, nao // YS, nemb), BF16),
            pltpu.VMEM((CHUNKS, ZS * XS) + unit, BF16),
            pltpu.VMEM((CHUNKS, ZS * XS) + unit, F32),
            pltpu.VMEM((CHUNKS, ZS * XS) + unit, BF16),
            pltpu.VMEM((CHUNKS,) + unit, BF16),
            pltpu.VMEM((CHUNKS,) + unit, BF16),
            pltpu.VMEM((CHUNKS, XS) + unit, BF16),
            pltpu.VMEM((CHUNKS, XS) + unit, BF16),
            pltpu.VMEM((CHUNKS,) + unit, BF16),
            pltpu.VMEM((2 * YS, CHUNKS) + unit, BF16),
            pltpu.VMEM((2 * YS, 2 * nemb, 2 * depth), BF16),
            pltpu.SemaphoreType.DMA((SLOTS,)),
            pltpu.SemaphoreType.DMA((NKA + YS - 2,)),
            pltpu.SemaphoreType.DMA((NKA + YS - 2,)),
            pltpu.SemaphoreType.DMA((KINDS, CHUNKS)),
            pltpu.SemaphoreType.DMA((KINDS, CHUNKS)),
            pltpu.SemaphoreType.DMA,
        ],
        compiler_params=pltpu.CompilerParams(
            collective_id=0, has_side_effects=True, vmem_limit_bytes=67_000_000
        ),
    )(orbital_coef, tensor, shifted_index)


def solution(mesh):
    placed = (P(None, "ka", None, None), P(None, "ka", None, None, "aux"), P())
    return jax.shard_map(
        local, mesh=mesh, in_specs=placed, out_specs=P(None, "ka", "aux"), check_vma=False
    )
```

```python
import functools

import jax
import jax.numpy as jnp
from jax import lax
from jax.experimental import pallas as pl
from jax.experimental.pallas import tpu as pltpu
from jax.sharding import PartitionSpec as P

F32, BF16 = jnp.float32, jnp.bfloat16
MESH = pl.DeviceIdType.MESH
ROWS = 16
CHUNKS = 8
SLOTS = 3
PICK_AT = 9
UNROLL = 8
CORES, ZS, XS, YS = 2, 4, 2, 4
NKA = CORES * ZS * XS
KINDS = 17


def matmul(left, right):
    return lax.dot_general(left, right, (((1,), (0,)), ((), ())), preferred_element_type=F32)


def matmul_nt(left, right):
    return lax.dot_general(left, right, (((1,), (1,)), ((), ())), preferred_element_type=F32)


def kernel(coef, tensor, index, out, blocks, turned, raw, w1f, w1, w2, half, cg, cs, away, mine, other, za, zb, zm, zp, xr, fg, cols,
           lsem, gsend, grecv, dsend, drecv, local_sem):
    nao = coef.shape[2]
    part = nao // YS
    nblocks = nao // ROWS
    ka, aux = lax.axis_index("ka"), lax.axis_index("aux")
    core, z, x = lax.rem(ka, CORES), lax.rem(lax.div(ka, CORES), ZS), lax.div(ka, CORES * ZS)
    y, xh = lax.rem(aux, YS), lax.div(aux, YS)
    up, down, across = lax.rem(z + 1, ZS), lax.rem(z + ZS - 1, ZS), lax.rem(z + 2, ZS)
    y_up, y_down = lax.rem(y + 1, YS), lax.rem(y + YS - 1, YS)
    aux_far = lax.rem(aux + YS, 2 * YS)
    to_core = (ka + 1 - 2 * core, aux)
    to_x = (lax.rem(ka + CORES * ZS, XS * CORES * ZS), aux)
    to_up = (x * CORES * ZS + up * CORES + core, aux)
    to_down = (x * CORES * ZS + down * CORES + core, aux)
    to_y_up, to_y_down = (ka, xh * YS + y_up), (ka, xh * YS + y_down)
    to_far = (ka, aux_far)
    x_other = 1 - x

    def load(i):
        return pltpu.make_async_copy(tensor.at[:, :, pl.ds(pl.multiple_of(i * ROWS, ROWS), ROWS), :], blocks.at[lax.rem(i, SLOTS)], lsem.at[lax.rem(i, SLOTS)])

    for i in range(SLOTS - 1):
        load(i).start()

    barrier = pltpu.get_barrier_semaphore()
    to_ka = [(lax.rem(ka + n, NKA), aux) for n in range(1, NKA)]
    to_ys = [(ka, xh * YS + lax.rem(y + n, YS)) for n in range(1, YS)]
    partners = to_ka + to_ys + [to_far]
    for partner in partners:
        pl.semaphore_signal(barrier, inc=1, device_id=partner, device_id_type=MESH)

    def send(src, dst, send_sem, recv_sem, where):
        return pltpu.make_async_remote_copy(
            src_ref=src, dst_ref=dst, send_sem=send_sem, recv_sem=recv_sem, device_id=where, device_id_type=MESH
        )

    own_rows = coef.at[:, 0, pl.ds(pl.multiple_of(y * part, 16), part), :]
    keep = pltpu.make_async_copy(own_rows, cg.at[ka], local_sem)
    spread = [send(own_rows, cg.at[ka], gsend.at[n], grecv.at[n], where) for n, where in enumerate(to_ka)]
    collect = [
        send(cs.at[y], cs.at[y], gsend.at[NKA - 1 + n], grecv.at[NKA - 1 + n], where) for n, where in enumerate(to_ys)
    ]
    keep.start()
    left_real, left_imag = coef[0, 0], coef[1, 0]
    left = jnp.concatenate(
        [jnp.concatenate([left_real, -left_imag], 1), jnp.concatenate([left_imag, left_real], 1)], 0
    ).T.astype(F32)
    for k in range(3):
        w1f[k] = left[:, k * 128 : k * 128 + 128]
    for h in range(2):
        for n in range(8):
            rows = pl.ds((n // 4) * 128 + h * 4 + n % 4, 16, stride=8)
            w1[h, n * 16 : n * 16 + 16] = jnp.concatenate([w1f[k, rows, :] for k in range(3)], 1).astype(BF16)

    def transform(h, i):
        for n in range(0, ROWS, 2):
            got = matmul(w1[h], jnp.concatenate([turned[i, n], turned[i, n + 1]], 1)).astype(BF16)
            raw[n] = got[:, :128]
            raw[n + 1] = got[:, 128:]
        at = pl.ds(pl.multiple_of(i * ROWS, ROWS), ROWS)
        for m in range(0, 128, 16):
            half[h, m : m + 16, at, :] = jnp.swapaxes(raw[:, m : m + 16, :], 0, 1)

    def first(i, carry):
        @pl.when(i == PICK_AT)
        def _():
            keep.wait()
            for copy in spread:
                copy.wait()
            cs[y] = cg[index[ka]]
            for copy in collect:
                copy.start()

        @pl.when(i + SLOTS - 1 < nblocks)
        def _():
            load(i + SLOTS - 1).start()

        load(i).wait()
        for c in range(2):
            for m in range(0, nao, 16):
                piece = blocks[lax.rem(i, SLOTS), c, m : m + 16]
                turned[i, :, c * nao + m : c * nao + m + 16, :] = jnp.swapaxes(piece, 0, 1)
        transform(0, i)
        return carry

    first(0, 0)
    pl.semaphore_wait(barrier, len(partners))
    for copy in spread:
        copy.start()
    lax.fori_loop(1, nblocks, first, 0)

    for copy in collect:
        copy.wait()
    right_real = jnp.concatenate([cs[n, 0] for n in range(YS)], 0)
    right_imag = jnp.concatenate([cs[n, 1] for n in range(YS)], 0)
    w2[...] = jnp.concatenate(
        [jnp.concatenate([right_real, right_imag], 1), jnp.concatenate([-right_imag, right_real], 1)], 0
    ).T

    def second(begin, end):
        def one(i, carry):
            transform(1, i)
            return carry

        lax.fori_loop(begin, end, one, 0)

    def pairs(cc, target, into):
        def one(q, carry):
            t = lax.rem(q, 2) * 8 + lax.div(q, 2) * 2 + target
            sides = []
            for c in (2 * cc, 2 * cc + 1):
                row = c % 4 * 16 + t
                sides.append(jnp.concatenate([half[c // 4, row], half[c // 4, 64 + row]], 0))
            got = matmul(w2[...], jnp.concatenate(sides, 1)).astype(into.dtype)
            into[2 * cc, q] = got[:, :128]
            into[2 * cc + 1, q] = got[:, 128:]
            return carry

        lax.fori_loop(0, 8, one, 0, unroll=UNROLL)

    def add(dst, srcs, scale=None):
        def one(i, carry):
            at = pl.ds(pl.multiple_of(i * 64, 64), 64)
            total = srcs[0][at]
            for src in srcs[1:]:
                total = total + src[at].astype(F32)
            if scale is not None:
                total = total * scale
            dst[at] = total.astype(BF16)
            return carry

        lax.fori_loop(0, 4, one, 0)

    def move(kind, c):
        def one(src, dst, where):
            return send(src, dst, dsend.at[kind, c], drecv.at[kind, c], where)

        if kind == 0:
            both = pl.ds(2 * c, 2)
            return one(away.at[both], other.at[both], to_core)
        if kind == 1:
            return one(other.at[c, across * 2], za.at[c], to_up)
        if kind == 2:
            return one(other.at[c, across * 2 + 1], zb.at[c], to_down)
        if kind in (3, 5):
            n = 1 if kind == 3 else 0
            return one(other.at[c, up * 2 + n], zm.at[c, n], to_up)
        if kind in (4, 6):
            n = 0 if kind == 4 else 1
            return one(other.at[c, down * 2 + n], zp.at[c, n], to_down)
        if kind == 7:
            return one(other.at[c, z * 2 + x_other], xr.at[c], to_x)
        low, high = pl.ds(0, 128), pl.ds(128, 128)
        if kind == 8:
            return one(fg.at[aux, c], fg.at[aux, c], to_far)
        if kind in (9, 10):
            return one(fg.at[aux, c], fg.at[aux, c], to_y_up if kind == 9 else to_y_down)
        if kind in (11, 12):
            return one(fg.at[aux_far, c], fg.at[aux_far, c], to_y_up if kind == 11 else to_y_down)
        base = (xh if kind < 15 else 1 - xh) * YS
        if kind in (13, 15):
            piece = fg.at[base + y_down, c, low]
            return one(piece, piece, to_y_up)
        piece = fg.at[base + y_up, c, high]
        return one(piece, piece, to_y_down)

    def pair_away(cc):
        pairs(cc, 1 - core, away)
        move(0, cc).start()

    def pair_mine(cc):
        pairs(cc, core, mine)

    def wait_core(cc):
        move(0, cc).wait_recv()

    def stage_a(c):
        for kind, q in ((1, across * 2), (2, across * 2 + 1)):
            add(other.at[c, q], (mine.at[c, q], other.at[c, q]))
            move(kind, c).start()

    def stage_a2(c):
        for kind, q in ((3, up * 2 + 1), (4, down * 2)):
            add(other.at[c, q], (mine.at[c, q], other.at[c, q]))
            move(kind, c).start()

    def stage_b(c):
        for first_kind, kind, q, got in ((1, 5, up * 2, za), (2, 6, down * 2 + 1, zb)):
            move(first_kind, c).wait_recv()
            add(other.at[c, q], (mine.at[c, q], other.at[c, q], got.at[c]))
            move(kind, c).start()

    def stage_d(c):
        for kind in (3, 4, 5, 6):
            move(kind, c).wait_recv()
        q = z * 2 + x_other
        add(other.at[c, q], (mine.at[c, q], other.at[c, q], zm.at[c, x_other], zp.at[c, x_other]))
        move(7, c).start()

    def stage_e(c):
        move(7, c).wait_recv()
        q = z * 2 + x
        add(fg.at[aux, c], (mine.at[c, q], other.at[c, q], zm.at[c, x], zp.at[c, x], xr.at[c]), 1 / (CORES * ZS * XS))
        for kind in (8, 9, 10):
            move(kind, c).start()

    def stage_g(c):
        move(8, c).wait_recv()
        move(11, c).start()
        move(12, c).start()

    def stage_h(c):
        for wait_kind, kind in ((9, 13), (10, 14)):
            move(wait_kind, c).wait_recv()
            move(kind, c).start()

    def stage_h2(c):
        for wait_kind, kind in ((11, 15), (12, 16)):
            move(wait_kind, c).wait_recv()
            move(kind, c).start()

    def stage_i(c):
        for kind in (13, 14, 15, 16):
            move(kind, c).wait_recv()

    pair_away(0)
    pair_mine(0)
    second(0, 1)
    pair_away(1)
    second(1, 2)
    pair_mine(1)
    wait_core(0)
    stage_a(0)
    stage_a2(0)
    second(2, 4)
    stage_a(1)
    second(4, 5)
    wait_core(1)
    second(5, 6)
    stage_a(2)
    second(6, 7)
    stage_b(0)
    second(7, 10)
    stage_a2(1)
    second(10, 12)
    stage_b(1)
    pair_away(2)
    pair_mine(2)
    stage_a2(2)
    stage_b(2)
    pair_away(3)
    stage_d(0)
    pair_mine(3)
    wait_core(2)
    stage_a(3)
    stage_d(1)
    stage_a(4)
    wait_core(3)
    stage_e(0)
    stage_a2(3)
    stage_d(2)
    stage_a2(4)
    stage_e(1)
    stage_b(3)
    stage_h(0)
    stage_b(4)
    stage_e(2)
    stage_h(1)
    stage_a(5)
    stage_g(0)
    stage_a2(5)
    stage_d(3)
    stage_g(1)
    stage_h(2)
    stage_a(6)
    stage_d(4)
    stage_a2(6)
    stage_g(2)
    stage_h2(0)
    stage_b(5)
    stage_e(3)
    stage_h2(1)
    stage_a(7)
    stage_e(4)
    stage_b(6)
    stage_h2(2)
    stage_a2(7)
    stage_h(3)
    stage_d(5)
    stage_g(3)
    stage_b(7)
    stage_h(4)
    stage_g(4)
    stage_d(6)
    stage_e(5)
    stage_h2(3)
    stage_d(7)
    stage_e(6)
    stage_h2(4)
    stage_h(5)
    stage_e(7)
    stage_h(6)
    stage_g(5)
    stage_g(6)
    stage_h(7)
    stage_g(7)
    stage_h2(5)
    stage_h2(6)
    stage_h2(7)
    for c in range(CHUNKS):
        stage_i(c)

    for j in range(2 * YS):
        column = fg[j, aux]
        real, imag = column[:128], column[128:]
        cols[j] = jnp.concatenate(
            [jnp.concatenate([real, imag], 1), jnp.concatenate([-imag, real], 1)], 0
        )

    def tile(i, carry):
        total = jnp.zeros((256, 256), F32)
        for j in range(2 * YS):
            rows = jnp.concatenate(
                [jnp.concatenate([fg[j, 2 * i + n, :128], fg[j, 2 * i + n, 128:]], 1) for n in range(2)], 0
            )
            total = total + matmul_nt(rows, cols[j])
        at = pl.ds(pl.multiple_of(i * 256, 256), 256)
        out[0, at, :] = total[:, :128]
        out[1, at, :] = total[:, 128:]
        return carry

    lax.fori_loop(0, CHUNKS // 2, tile, 0, unroll=2)

    for kind in range(KINDS):
        for c in range(CHUNKS if kind else CHUNKS // 2):
            move(kind, c).wait_send()


def local(orbital_coef, dftensor, shifted_index):
    nao, nemb = orbital_coef.shape[2:]
    depth = dftensor.shape[-1]
    tensor = dftensor.reshape(2, nao, nao, depth)
    unit = (2 * nemb, depth)
    return pl.pallas_call(
        kernel,
        out_shape=jax.ShapeDtypeStruct((2, 8 * nemb, nemb), F32),
        in_specs=[
            pl.BlockSpec(memory_space=pltpu.VMEM),
            pl.BlockSpec(memory_space=pl.ANY),
            pl.BlockSpec(memory_space=pltpu.SMEM),
        ],
        out_specs=pl.BlockSpec(memory_space=pltpu.VMEM),
        scratch_shapes=[
            pltpu.VMEM((SLOTS, 2, nao, ROWS, depth), BF16),
            pltpu.VMEM((nao // ROWS, ROWS, 2 * nao, depth), BF16),
            pltpu.VMEM((ROWS, nemb, depth), BF16),
            pltpu.VMEM((3, 2 * nemb, 128), F32),
            pltpu.VMEM((2, nemb, 2 * nao), BF16),
            pltpu.VMEM((2 * nemb, 2 * nao), BF16),
            pltpu.VMEM((2, nemb, nao, depth), BF16),
            pltpu.VMEM((CORES * ZS * XS, 2, nao // YS, nemb), BF16),
            pltpu.VMEM((YS, 2, nao // YS, nemb), BF16),
            pltpu.VMEM((CHUNKS, ZS * XS) + unit, BF16),
            pltpu.VMEM((CHUNKS, ZS * XS) + unit, F32),
            pltpu.VMEM((CHUNKS, ZS * XS) + unit, BF16),
            pltpu.VMEM((CHUNKS,) + unit, BF16),
            pltpu.VMEM((CHUNKS,) + unit, BF16),
            pltpu.VMEM((CHUNKS, XS) + unit, BF16),
            pltpu.VMEM((CHUNKS, XS) + unit, BF16),
            pltpu.VMEM((CHUNKS,) + unit, BF16),
            pltpu.VMEM((2 * YS, CHUNKS) + unit, BF16),
            pltpu.VMEM((2 * YS, 2 * nemb, 2 * depth), BF16),
            pltpu.SemaphoreType.DMA((SLOTS,)),
            pltpu.SemaphoreType.DMA((NKA + YS - 2,)),
            pltpu.SemaphoreType.DMA((NKA + YS - 2,)),
            pltpu.SemaphoreType.DMA((KINDS, CHUNKS)),
            pltpu.SemaphoreType.DMA((KINDS, CHUNKS)),
            pltpu.SemaphoreType.DMA,
        ],
        compiler_params=pltpu.CompilerParams(
            collective_id=0, has_side_effects=True, vmem_limit_bytes=67_000_000
        ),
    )(orbital_coef, tensor, shifted_index)


def solution(mesh):
    placed = (P(None, "ka", None, None), P(None, "ka", None, None, "aux"), P())
    return jax.shard_map(
        local, mesh=mesh, in_specs=placed, out_specs=P(None, "ka", "aux"), check_vma=False
    )
```
